32 devices in a mesh: groups: 2 (over y), section: 4 (over z), replica: 4 (over x, core).
Axes of the slice: x: 2, y: 2, z: 4, core: 2. Of those that a mesh axis runs over, the one named last changes fastest.
Arguments:
- section_inputs: bfloat16 [8, 4, 2, 16, 16, 256], P(('groups', 'replica'), 'section'), parts along dimension 0, may hold values from -6 to 6
- cotangent: bfloat16 [8, 2, 16, 16, 256], P(('groups', 'replica')), parts along dimension 0, may hold values from -6 to 6
- crop_rows: int32 [8, 2], P(('groups', 'replica')), parts along dimension 0, may hold values from 0 to 705
- drift: bfloat16 [8, 4, 9, 256, 256], P(('groups', 'replica'), 'section'), parts along dimension 0, may hold values from -6 to 6
- params: float32 [8, 9, 256, 256], P(('groups', 'section')), parts along dimension 0, may hold values from -6 to 6
- momentum: float32 [8, 9, 256, 256], P(('groups', 'section'), None, 'replica'), parts along dimension 0, may hold values from -4 to 4
Outputs:
- new_params: float32 [8, 9, 256, 256], P(('groups', 'section')), parts along dimension 0
- new_momentum: float32 [8, 9, 256, 256], P(('groups', 'section'), None, 'replica'), parts along dimension 0
The draws below stay inside these ranges and needn't reach their ends.
There are 2 independent parts, one for each index of `groups`. The reference program is written for one: setup_inputs(seed, part) draws one part's arguments, and reference() takes and returns one part's arrays. A program takes and returns all parts, laid end to end along the dimension named above; each array names one. Nothing has to cross between parts.
All inputs are finite; a program needn't handle non-finite values.
Results may differ from the reference program's by a relative error of at most 0.0075.
Values may be sent and summed in bfloat16 or wider, within the bound.
No kernel may reach another device: no remote copies, remote signals or barrier semaphores. Data moves between devices by JAX's collectives and lax.ppermute only.
A program may use at most 64 MiB of HBM per device.

```python
import math
import jax
import jax.numpy as jnp
from jax import lax

CH = 256
TAPS = 9
LATS = 721
ROWS = 16
COLS = 16
MB = 2
SECTIONS = 4
REPLICAS = 4


def set_ends(result, key, smallest, largest):
    shape = result.shape
    place = [jax.random.randint(jax.random.fold_in(key, axis), (), 0, shape[axis]) for axis in range(len(shape))]
    result = result.at[tuple(place)].set(smallest)
    longest = shape.index(max(shape))
    place[longest] = (place[longest] + 1) % shape[longest]
    return result.at[tuple(place)].set(largest)


def strengthened(entries, rng, source, target, parts, factor):
    def block_of(axis_at):
        return (jnp.arange(entries.shape[axis_at]) // (entries.shape[axis_at] // parts)).reshape((-1,) + (1,) * (entries.ndim - 1 - axis_at))

    near = jax.random.permutation(rng, parts)[block_of(target)]
    other_side = (block_of(target) + parts // 2) % parts
    return jnp.where((block_of(source) == near) | (block_of(source) == other_side), factor * entries, entries)


def block_scale(own_key, shape, split, smallest, top_value):
    def one(position, shards_of):
        draws = jax.random.uniform(jax.random.fold_in(jax.random.fold_in(own_key, 6), position), (shards_of,), jnp.float32, smallest / len(split), top_value / len(split))
        return jnp.repeat(jnp.exp(draws), shape[position] // shards_of).reshape((-1,) + (1,) * (len(shape) - position - 1))

    gain = one(*split[0])
    for cut in split[1:]:
        gain = gain * one(*cut)
    return gain


def bell_draw(stream_key, shape, deviation, limit, cuts=(), kind=jnp.bfloat16):
    factor_of = block_scale(stream_key, shape, cuts, -0.22, 0.18) if cuts else 1.0
    entries = jax.random.normal(stream_key, shape, jnp.float32) * deviation * factor_of
    return jnp.minimum(jnp.maximum(entries, -limit), limit).astype(kind)


def heavy_noise(stream_key, extent, deviation, limit, pieces, heavy, kind=jnp.bfloat16):
    entries = deviation * jax.random.normal(stream_key, extent, jnp.float32)
    if pieces:
        entries = entries * block_scale(stream_key, extent, pieces, -0.22, 0.18)
    return jnp.clip(strengthened(entries, jax.random.fold_in(stream_key, 3), *heavy), -limit, limit).astype(kind)


def setup_inputs(seed: int = 0, part: int = 0) -> dict:
    key_of = jax.random.split(jax.random.key(seed), 7)
    own_keys = jax.random.split(jax.random.fold_in(key_of[6], part), 7)
    section_inputs = bell_draw(own_keys[0], (REPLICAS, SECTIONS, MB, ROWS, COLS, CH), 1.0, 6.0, ((0, 4), (1, 4)))
    cotangent = bell_draw(own_keys[1], (REPLICAS, MB, ROWS, COLS, CH), 1.0, 6.0, ((0, 4),))
    crop_rows = set_ends(jax.random.randint(own_keys[2], (REPLICAS, MB), 0, LATS - ROWS + 1), jax.random.fold_in(own_keys[2], 1), 0, LATS - ROWS).astype(jnp.int32)
    drift = heavy_noise(own_keys[3], (REPLICAS, SECTIONS, TAPS, CH, CH), 0.3, 6.0, ((0, 4), (1, 4)), (0, 3, 4, 2.0))
    params = bell_draw(own_keys[4], (SECTIONS, TAPS, CH, CH), 1.0, 6.0, ((0, 4),), jnp.float32)
    momentum = bell_draw(own_keys[5], (SECTIONS, TAPS, CH, CH), 0.3, 4.0, ((0, 4), (2, 4)), jnp.float32)
    return {"section_inputs": section_inputs, "cotangent": cotangent, "crop_rows": crop_rows, "drift": drift, "params": params, "momentum": momentum}


def lat_weight(first_row, count):
    rows = jnp.arange(count, dtype=jnp.float32) + first_row.astype(jnp.float32)
    middle = (LATS - 1) / 2.0
    every = jnp.arange(LATS, dtype=jnp.float32)
    norm_value = jnp.mean(jnp.cos(math.pi * (every - middle) / (LATS - 1)))
    return jnp.cos(math.pi * (rows - middle) / (LATS - 1)) / norm_value


def backward(inputs, out_grad, weights):
    rows, cols, width = inputs.shape
    scale = (9.0 * width) ** -0.5
    padded = jnp.pad(inputs, ((1, 1), (1, 1), (0, 0))).astype(jnp.float32)
    taps = jnp.stack([padded[a:a + rows, b:b + cols] for a in range(3) for b in range(3)])
    wide = weights.astype(jnp.float32)
    pre = jnp.einsum('krcd,kde->rce', taps, wide) * scale
    tangent = jnp.tanh(pre)
    local = (out_grad.astype(jnp.float32) * (1.0 - tangent * tangent)).astype(jnp.bfloat16)
    local_wide = local.astype(jnp.float32)
    grad = jnp.einsum('krcd,rce->kde', taps, local_wide) * scale
    back = jnp.einsum('rce,kde->krcd', local_wide, wide)
    accum = jnp.zeros((rows + 2, cols + 2, width), jnp.float32)
    for a in range(3):
        for b in range(3):
            accum = accum.at[a:a + rows, b:b + cols].add(back[3 * a + b])
    in_grad = (out_grad.astype(jnp.float32) + scale * accum[1:rows + 1, 1:cols + 1]).astype(jnp.bfloat16)
    return grad, in_grad


def reference(section_inputs, cotangent, crop_rows, drift, params, momentum):
    weights_bf = params.astype(jnp.bfloat16)

    def one_replica(items):
        inputs_here, cot_here, crops_here = items
        grads = [jnp.zeros((TAPS, CH, CH), jnp.float32) for section in range(SECTIONS)]
        for micro in range(MB):
            weight_rows = lat_weight(crops_here[micro], ROWS)
            carried = (cot_here[micro].astype(jnp.float32) * weight_rows[:, None, None]).astype(jnp.bfloat16)
            for section in reversed(range(SECTIONS)):
                contrib, carried = backward(inputs_here[section, micro], carried, weights_bf[section])
                grads[section] = grads[section] + contrib
        return jnp.stack(grads)

    weight_grad = lax.map(one_replica, (section_inputs, cotangent, crop_rows))
    delta = (drift.astype(jnp.float32) + 0.5 * weight_grad).astype(jnp.bfloat16)
    delta = lax.optimization_barrier(delta)
    mean_delta = jnp.sum(delta.astype(jnp.float32), axis=0) / REPLICAS
    new_momentum = 0.9 * momentum + mean_delta
    new_params = params - 0.7 * (mean_delta + 0.9 * new_momentum)
    return new_params, new_momentum
```

```python
import functools
import math

import jax
import jax.numpy as jnp
import numpy as np
from jax import lax
from jax.experimental import pallas as pl
from jax.experimental.pallas import tpu as pltpu
from jax.sharding import PartitionSpec as P

LATS = 721
MIDDLE = (LATS - 1) / 2.0
NORM = float(np.mean(np.cos(math.pi * (np.arange(LATS) - MIDDLE) / (LATS - 1))))
F32 = jnp.float32
BF16 = jnp.bfloat16
NN = (((1,), (0,)), ((), ()))
NT = (((1,), (1,)), ((), ()))
VMEM_LIMIT = 24 << 20


def params_of(**more):
    return pltpu.CompilerParams(vmem_limit_bytes=VMEM_LIMIT, **more)


def spread(ref, at, values, rows, cols):
    length = rows * cols
    column = lax.broadcasted_iota(jnp.int32, values.shape, 0) % cols
    zeros = jnp.zeros((cols, values.shape[1]), BF16)
    for b in range(3):
        if b == 0:
            moved = jnp.where(column == 0, 0.0, pltpu.roll(values, 1, 0))
        elif b == 2:
            moved = jnp.where(column == cols - 1, 0.0, pltpu.roll(values, length - 1, 0))
        else:
            moved = values
        ref[(*at, b, pl.ds(0, cols), slice(None))] = zeros
        ref[(*at, b, pl.ds(cols, length), slice(None))] = moved.astype(BF16)
        ref[(*at, b, pl.ds(cols + length, cols), slice(None))] = zeros


def prepare(crop_rows, inputs, cotangent, weights, rows, cols):
    micro, length, width = inputs.shape
    taps = weights.shape[0]
    scale = (9.0 * width) ** (-0.5)

    def kernel(scalars, x_ref, cot_ref, w_ref, wbf_ref, slope_ref, top_ref, shifted, total):
        step = pl.program_id(0)

        @pl.when(step == 0)
        def _():
            for m in range(micro):
                spread(shifted, (m,), x_ref[m].astype(F32), rows, cols)
                here = lax.broadcasted_iota(jnp.int32, (rows, 128), 0) + scalars[m]
                angle = math.pi * (here.astype(F32) - MIDDLE) / (LATS - 1)
                factor = jnp.cos(angle) / NORM
                factor = jnp.where(scalars[micro] == 1, factor, 0.0)
                for i in range(rows):
                    line = jnp.concatenate([jnp.broadcast_to(factor[i : i + 1], (cols, 128))] * (width // 128), axis=1)
                    part = cot_ref[m, i * cols : (i + 1) * cols, :].astype(F32)
                    top_ref[m, i * cols : (i + 1) * cols, :] = (part * line).astype(BF16)
            total[...] = jnp.zeros_like(total)

        tap = w_ref[0].astype(BF16)
        wbf_ref[0] = tap
        a, b = step // 3, step % 3
        start = pl.multiple_of(a * cols, cols)
        for m in range(micro):
            total[m] += lax.dot_general(
                shifted[m, b, pl.ds(start, length), :], tap, NN, preferred_element_type=F32
            )

        @pl.when(step == taps - 1)
        def _():
            tangent = jnp.tanh(total[...] * scale)
            slope_ref[...] = 1.0 - tangent * tangent

    whole = lambda k, s: (0, 0, 0)
    return pl.pallas_call(
        kernel,
        out_shape=(
            jax.ShapeDtypeStruct((taps, width, width), BF16),
            jax.ShapeDtypeStruct((micro, length, width), F32),
            jax.ShapeDtypeStruct((micro, length, width), BF16),
        ),
        grid_spec=pltpu.PrefetchScalarGridSpec(
            num_scalar_prefetch=1,
            grid=(taps,),
            in_specs=[
                pl.BlockSpec((micro, length, width), whole),
                pl.BlockSpec((micro, length, width), whole),
                pl.BlockSpec((1, width, width), lambda k, s: (k, 0, 0)),
            ],
            out_specs=[
                pl.BlockSpec((1, width, width), lambda k, s: (k, 0, 0)),
                pl.BlockSpec((micro, length, width), whole),
                pl.BlockSpec((micro, length, width), whole),
            ],
            scratch_shapes=[
                pltpu.VMEM((micro, 3, length + 2 * cols, width), BF16),
                pltpu.VMEM((micro, length, width), F32),
            ],
        ),
        compiler_params=params_of(),
        name="prepare",
    )(crop_rows, inputs, cotangent, weights)


def stage(arrived, slope, weights, rows, cols):
    taps, width, _ = weights.shape
    length = rows * cols
    scale = (9.0 * width) ** (-0.5)
    count = len(arrived)

    def kernel(*refs):
        parts, (slope_ref, w_ref, out_ref, shifted) = refs[:count], refs[count:]
        grad = parts[0][...].astype(F32)
        for part in parts[1:]:
            grad += part[...].astype(F32)
        local = (grad * slope_ref[...]).astype(BF16).astype(F32)
        spread(shifted, (), local, rows, cols)
        total = None
        for a in range(3):
            for b in range(3):
                at = (2 - a) * cols
                term = lax.dot_general(
                    shifted[2 - b, at : at + length, :], w_ref[3 * a + b], NT, preferred_element_type=F32
                )
                total = term if total is None else total + term
        out_ref[...] = (grad + scale * total).astype(BF16)

    return pl.pallas_call(
        kernel,
        out_shape=jax.ShapeDtypeStruct((length, width), BF16),
        in_specs=[pl.BlockSpec(memory_space=pltpu.VMEM)] * (count + 2),
        out_specs=pl.BlockSpec(memory_space=pltpu.VMEM),
        scratch_shapes=[pltpu.VMEM((3, length + 2 * cols, width), BF16)],
        compiler_params=params_of(),
        name="stage",
    )(*arrived, slope, weights)


def turned_taps(inputs, rows, cols):
    blocks, length, width = inputs.shape

    def kernel(x_ref, out_ref, shifted):
        spread(shifted, (), x_ref[0].astype(F32), rows, cols)
        for a in range(3):
            for b in range(3):
                out_ref[0, 3 * a + b] = shifted[b, a * cols : a * cols + length, :].T

    return pl.pallas_call(
        kernel,
        grid=(blocks,),
        out_shape=jax.ShapeDtypeStruct((blocks, 9, width, length), BF16),
        in_specs=[pl.BlockSpec((1, length, width), lambda n: (n, 0, 0))],
        out_specs=pl.BlockSpec((1, 9, width, length), lambda n: (n, 0, 0, 0)),
        scratch_shapes=[pltpu.VMEM((3, length + 2 * cols, width), BF16)],
        compiler_params=params_of(),
        name="turned_taps",
    )(inputs)


def contract(base, momentum_base, turned, local, here, gains):
    taps, width, _ = base.shape
    share = momentum_base.shape[1]
    blocks, length, _ = local.shape

    def kernel(scalars, base_ref, mom_ref, t_ref, l_ref, out_ref, mom_out_ref, total):
        acc = None
        for n in range(blocks):
            term = lax.dot_general(t_ref[n, 0], l_ref[n], NN, preferred_element_type=F32)
            acc = term if acc is None else acc + term
        total[...] = acc
        out_ref[0] = base_ref[0] + gains[0] * acc
        own = total[pl.ds(pl.multiple_of(scalars[0], share), share), :]
        mom_out_ref[0] = mom_ref[0] + gains[1] * own

    return pl.pallas_call(
        kernel,
        out_shape=(
            jax.ShapeDtypeStruct(base.shape, F32),
            jax.ShapeDtypeStruct(momentum_base.shape, F32),
        ),
        grid_spec=pltpu.PrefetchScalarGridSpec(
            num_scalar_prefetch=1,
            grid=(taps,),
            in_specs=[
                pl.BlockSpec((1, width, width), lambda k, s: (k, 0, 0)),
                pl.BlockSpec((1, share, width), lambda k, s: (k, 0, 0)),
                pl.BlockSpec((blocks, 1, width, length), lambda k, s: (0, k, 0, 0)),
                pl.BlockSpec((blocks, length, width), lambda k, s: (0, 0, 0)),
            ],
            out_specs=[
                pl.BlockSpec((1, width, width), lambda k, s: (k, 0, 0)),
                pl.BlockSpec((1, share, width), lambda k, s: (k, 0, 0)),
            ],
            scratch_shapes=[pltpu.VMEM((width, width), F32)],
        ),
        compiler_params=params_of(),
        name="contract",
    )(here, base, momentum_base, turned, local)


def per_device(section_inputs, cotangent, crop_rows, drift, params, momentum):
    section, sections = lax.axis_index("section"), lax.axis_size("section")
    here, replicas = lax.axis_index("replica"), lax.axis_size("replica")
    micro, rows, cols, width = section_inputs.shape[2:]
    length = rows * cols
    share = width // replicas
    taps = params.shape[1]
    scale = (9.0 * width) ** (-0.5)
    bits = [1 << n for n in reversed(range((replicas - 1).bit_length()))]
    x = section_inputs.reshape(micro, length, width)

    def swap(value, bit):
        return lax.ppermute(value, "replica", [(i, i ^ bit) for i in range(replicas)])

    def spread_out(value):
        held = [value]
        for bit in bits:
            held += [swap(one, bit) for one in held]
        return held

    def hop(value, step):
        return lax.ppermute(value, "section", [(sections - 1 - step, sections - 2 - step)])

    scalars = jnp.concatenate([crop_rows.reshape(-1), (section == sections - 1).astype(jnp.int32)[None]])
    weights, slope, top = prepare(
        scalars, x, cotangent.reshape(micro, length, width), params[0], rows, cols
    )
    arrived = [[top[m]] for m in range(micro)]
    for step in range(sections - 1):
        for m in range(micro):
            arrived[m].append(hop(stage(arrived[m], slope[m], weights, rows, cols), step))

    held_x = spread_out(x)

    part = drift.reshape(taps, replicas, share, width)
    order = [jnp.bitwise_xor(here, j) for j in range(replicas)]
    parts = [lax.dynamic_index_in_dim(part, order[j], 1, keepdims=False) for j in range(replicas)]
    live = {j: parts[j].astype(F32) for j in range(replicas)}
    for bit in reversed(bits):
        sent = {j: swap(v.astype(BF16), bit) for j, v in live.items() if j & bit}
        live = {j: v + sent[j | bit].astype(F32) for j, v in live.items() if not j & bit}
    drift_mean = live[0] / replicas

    own = momentum[0]
    advance = 1.33 * drift_mean + 0.567 * own
    pieces = spread_out(advance.astype(BF16))
    whole = jnp.zeros((taps, replicas, share, width), BF16)
    for j, piece in enumerate(pieces):
        q = 0
        for n, bit in enumerate(bits):
            if j >> n & 1:
                q |= bit
        whole = lax.dynamic_update_index_in_dim(whole, piece, jnp.bitwise_xor(here, q), 1)
    base = params[0] - whole.reshape(taps, width, width).astype(F32)
    momentum_base = 0.9 * own + drift_mean

    gain = 0.5 * scale / replicas
    gains = (-1.33 * gain, gain)
    start = (here * share).astype(jnp.int32)[None]
    for m in range(micro):
        local = sum(one.astype(F32) for one in arrived[m]) * slope[m]
        held_local = spread_out(local.astype(BF16))
        turned = turned_taps(jnp.stack([one[m] for one in held_x]), rows, cols)
        base, momentum_base = contract(
            base, momentum_base, turned, jnp.stack(held_local), start, gains
        )
    return (base[None], momentum_base[None])


def solution(mesh):
    placed = (
        P(("groups", "replica"), "section", None, None, None, None),
        P(("groups", "replica"), None, None, None, None),
        P(("groups", "replica"), None),
        P(("groups", "replica"), "section", None, None, None),
        P(("groups", "section"), None, None, None),
        P(("groups", "section"), None, "replica", None),
    )
    return jax.shard_map(
        per_device,
        mesh=mesh,
        in_specs=placed,
        out_specs=(
            P(("groups", "section"), None, None, None),
            P(("groups", "section"), None, "replica", None),
        ),
        check_vma=False,
    )
```

```python
import functools
import math

import jax
import jax.numpy as jnp
import numpy as np
from jax import lax
from jax.experimental import pallas as pl
from jax.experimental.pallas import tpu as pltpu
from jax.sharding import PartitionSpec as P

LATS = 721
MIDDLE = (LATS - 1) / 2.0
NORM = float(np.mean(np.cos(math.pi * (np.arange(LATS) - MIDDLE) / (LATS - 1))))
F32 = jnp.float32
BF16 = jnp.bfloat16
NN = (((1,), (0,)), ((), ()))
NT = (((1,), (1,)), ((), ()))
VMEM_LIMIT = 30 << 20
STAGE_WEIGHT = 8
VMEM = pl.BlockSpec(memory_space=pltpu.VMEM)
HBM = pl.BlockSpec(memory_space=pltpu.HBM)


def params_of(**more):
    return pltpu.CompilerParams(vmem_limit_bytes=VMEM_LIMIT, **more)


def spread(ref, at, values, rows, cols):
    length = rows * cols
    column = lax.broadcasted_iota(jnp.int32, values.shape, 0) % cols
    zeros = jnp.zeros((cols, values.shape[1]), BF16)
    for b in range(3):
        if b == 0:
            moved = jnp.where(column == 0, 0.0, pltpu.roll(values, 1, 0))
        elif b == 2:
            moved = jnp.where(column == cols - 1, 0.0, pltpu.roll(values, length - 1, 0))
        else:
            moved = values
        ref[(*at, b, pl.ds(0, cols), slice(None))] = zeros
        ref[(*at, b, pl.ds(cols, length), slice(None))] = moved.astype(BF16)
        ref[(*at, b, pl.ds(cols + length, cols), slice(None))] = zeros


def stay(value):
    return pltpu.with_memory_space_constraint(value, pltpu.HBM)


def after(value, *others):
    return lax.optimization_barrier((value, *others))[0]


def product_cost(count, length, width, moved):
    return pl.CostEstimate(flops=2 * count * length * width * width, bytes_accessed=moved, transcendentals=0)


def gradient_in(grad, local, shifted, w_ref, rows, cols):
    length, width = grad.shape
    spread(shifted, (), local, rows, cols)
    total = None
    for a in range(3):
        for b in range(3):
            at = (2 - a) * cols
            term = lax.dot_general(
                shifted[2 - b, at : at + length, :], w_ref[3 * a + b], NT, preferred_element_type=F32
            )
            total = term if total is None else total + term
    return grad + (9.0 * width) ** (-0.5) * total


def prepare(crop_rows, inputs, cotangent, weights, rows, cols):
    micro, length, width = inputs.shape
    taps = weights.shape[0]
    scale = (9.0 * width) ** (-0.5)

    def kernel(crop_ref, x_ref, cot_ref, w_ref, wbf_ref, x_now, *refs):
        slopes, tops, refs = refs[:micro], refs[micro : 2 * micro], refs[2 * micro :]
        cot_now, crop_now, shifted, w_now, sems = refs
        load_x = pltpu.make_async_copy(x_ref, x_now, sems.at[0])
        load_cot = pltpu.make_async_copy(cot_ref, cot_now, sems.at[1])
        load_crop = pltpu.make_async_copy(crop_ref, crop_now, sems.at[2])
        loads = [pltpu.make_async_copy(w_ref.at[k], w_now.at[k], sems.at[3 + k]) for k in range(taps)]
        for load in (load_crop, load_x, *loads, load_cot):
            load.start()
        load_crop.wait()
        is_last = lax.axis_index("section") == lax.axis_size("section") - 1
        factors = []
        for m in range(micro):
            here = lax.broadcasted_iota(jnp.int32, (rows, 128), 0) + crop_now[0, m]
            factor = jnp.cos(math.pi * (here.astype(F32) - MIDDLE) / (LATS - 1)) / NORM
            factors.append(jnp.where(is_last, factor, 0.0))
        load_x.wait()
        for m in range(micro):
            spread(shifted, (m,), x_now[m].astype(F32), rows, cols)

        def product(m, k, total):
            a, b = divmod(k, 3)
            term = lax.dot_general(
                shifted[m, b, a * cols : a * cols + length, :], wbf_ref[k], NN, preferred_element_type=F32
            )
            return term if total is None else total + term

        total = None
        for k in range(taps):
            loads[k].wait()
            wbf_ref[k] = w_now[k].astype(BF16)
            total = product(0, k, total)
        for m in range(micro):
            if m:
                total = None
                for k in range(taps):
                    total = product(m, k, total)
            else:
                load_cot.wait()
            tangent = jnp.tanh(total * scale)
            slopes[m][...] = 1.0 - tangent * tangent
            for i in range(rows):
                line = jnp.broadcast_to(factors[m][i : i + 1], (cols, 128))
                line = jnp.concatenate([line] * (width // 128), axis=1)
                at = slice(i * cols, (i + 1) * cols)
                tops[m][at, :] = (cot_now[m, at, :].astype(F32) * line).astype(BF16)

    shapes = [jax.ShapeDtypeStruct(weights.shape, BF16), jax.ShapeDtypeStruct(inputs.shape, BF16)]
    shapes += [jax.ShapeDtypeStruct((length, width), F32)] * micro
    shapes += [jax.ShapeDtypeStruct((length, width), BF16)] * micro
    out = pl.pallas_call(
        kernel,
        out_shape=shapes,
        in_specs=[HBM] * 4,
        out_specs=[VMEM] * len(shapes),
        scratch_shapes=[
            pltpu.VMEM(inputs.shape, BF16),
            pltpu.SMEM(crop_rows.shape, jnp.int32),
            pltpu.VMEM((micro, 3, length + 2 * cols, width), BF16),
            pltpu.VMEM(weights.shape, F32),
            pltpu.SemaphoreType.DMA((3 + taps,)),
        ],
        compiler_params=params_of(),
        name="prepare",
    )(*[stay(one) for one in (crop_rows, inputs, cotangent, weights)])
    return out[0], out[1], out[2 : 2 + micro], out[2 + micro :]


def stage(arrived, slope, weights, rows, cols):
    taps, width, _ = weights.shape
    length = rows * cols
    count = len(arrived)

    def kernel(*refs):
        parts, (slope_ref, w_ref, out_ref, shifted) = refs[:count], refs[count:]
        grad = parts[0][...].astype(F32)
        for part in parts[1:]:
            grad += part[...].astype(F32)
        local = (grad * slope_ref[...]).astype(BF16).astype(F32)
        out_ref[...] = gradient_in(grad, local, shifted, w_ref, rows, cols).astype(BF16)

    return pl.pallas_call(
        kernel,
        out_shape=jax.ShapeDtypeStruct((length, width), BF16),
        in_specs=[VMEM] * (count + 2),
        out_specs=VMEM,
        scratch_shapes=[pltpu.VMEM((3, length + 2 * cols, width), BF16)],
        compiler_params=params_of(),
        cost_estimate=product_cost(STAGE_WEIGHT * taps, length, width, 2 * weights.size),
        name="stage",
    )(*arrived, slope, weights)


def turned_taps(inputs, rows, cols):
    blocks, length, width = inputs.shape

    def kernel(x_ref, out_ref, shifted):
        for n in range(blocks):
            spread(shifted, (), x_ref[n].astype(F32), rows, cols)
            for a in range(3):
                for b in range(3):
                    out_ref[n, 3 * a + b] = shifted[b, a * cols : a * cols + length, :].T

    return pl.pallas_call(
        kernel,
        out_shape=jax.ShapeDtypeStruct((blocks, 9, width, length), BF16),
        in_specs=[VMEM],
        out_specs=VMEM,
        scratch_shapes=[pltpu.VMEM((3, length + 2 * cols, width), BF16)],
        compiler_params=params_of(),
        name="turned_taps",
    )(inputs)


def outgoing(near, far, momentum, last, replicas):
    taps, width, _ = near.shape
    share = momentum.shape[1]

    def kernel(near_ref, far_ref, own_ref, out_ref, rest_ref, total):
        here = lax.axis_index("replica")
        own_rows = pl.ds(pl.multiple_of(here * share, share), share)
        other_rows = pl.ds(pl.multiple_of(jnp.bitwise_xor(here, last) * share, share), share)
        for k in range(taps):
            total[k % 2] = near_ref[k].astype(F32) + far_ref[k].astype(F32)
            mine = total[k % 2, own_rows, :]
            out_ref[k, :share] = (1.33 / replicas * mine + 0.567 * own_ref[k]).astype(BF16)
            out_ref[k, share:] = total[k % 2, other_rows, :].astype(BF16)
            rest_ref[k] = 0.9 * own_ref[k] + mine / replicas

    return pl.pallas_call(
        kernel,
        out_shape=(
            jax.ShapeDtypeStruct((taps, 2 * share, width), BF16),
            jax.ShapeDtypeStruct(momentum.shape, F32),
        ),
        in_specs=[VMEM] * 3,
        out_specs=[VMEM] * 2,
        scratch_shapes=[pltpu.VMEM((2, width, width), F32)],
        compiler_params=params_of(),
        name="outgoing",
    )(near, far, momentum)


def incoming(ours, theirs, rest, replicas):
    share = rest.shape[1]

    def kernel(ours_ref, theirs_ref, rest_ref, out_ref, momentum_ref):
        for k in range(rest.shape[0]):
            mine, there = ours_ref[k].astype(F32), theirs_ref[k].astype(F32)
            out_ref[k, :share] = (mine[:share] + 1.33 / replicas * there[share:]).astype(BF16)
            out_ref[k, share:] = (there[:share] + 1.33 / replicas * mine[share:]).astype(BF16)
            momentum_ref[k] = rest_ref[k] + there[share:] / replicas

    return pl.pallas_call(
        kernel,
        out_shape=(jax.ShapeDtypeStruct(ours.shape, BF16), jax.ShapeDtypeStruct(rest.shape, F32)),
        in_specs=[VMEM] * 3,
        out_specs=[VMEM] * 2,
        compiler_params=params_of(),
        name="incoming",
    )(ours, theirs, rest)


def contract(base, momentum_base, blocks, gains, final, pieces=(), last=0):
    taps, width, _ = base.shape
    share = momentum_base.shape[1]
    count = len(blocks)

    def kernel(base_ref, mom_ref, *refs):
        turned, local, refs = refs[:count], refs[count : 2 * count], refs[2 * count :]
        taken, refs = refs[: len(pieces)], refs[len(pieces) :]
        out_ref, mom_out_ref, total = refs[:3]
        if final:
            out_now, mom_now, sems = refs[3:]
        else:
            out_now, mom_now = out_ref, mom_out_ref
        here = lax.axis_index("replica")
        own = pl.multiple_of(here * share, share)
        copies = []
        for k in range(taps):
            acc = None
            for n in range(count):
                term = lax.dot_general(turned[n][blocks[n][1], k], local[n][...], NN, preferred_element_type=F32)
                acc = term if acc is None else acc + term
            total[k % 2] = acc
            out_now[k] = base_ref[k] + gains[0] * acc
            for (at, _), piece in zip(pieces, taken):
                for n in range(2):
                    where = jnp.bitwise_xor(here, at | n * last) * share
                    lines = pl.ds(pl.multiple_of(where, share), share)
                    out_now[k, lines, :] -= piece[k, n * share : (n + 1) * share].astype(F32)
            mom_now[k] = mom_ref[k] + gains[1] * total[k % 2, pl.ds(own, share), :]
            if final:
                copies.append(pltpu.make_async_copy(out_now.at[k], out_ref.at[k], sems.at[0, k]))
                copies.append(pltpu.make_async_copy(mom_now.at[k], mom_out_ref.at[k], sems.at[1, k]))
                copies[-2].start()
                copies[-1].start()
        for copy in copies:
            copy.wait()

    scratch = [pltpu.VMEM((2, width, width), F32)]
    if final:
        scratch += [
            pltpu.VMEM(base.shape, F32),
            pltpu.VMEM(momentum_base.shape, F32),
            pltpu.SemaphoreType.DMA((2, taps)),
        ]
    return pl.pallas_call(
        kernel,
        out_shape=(
            jax.ShapeDtypeStruct(base.shape, F32),
            jax.ShapeDtypeStruct(momentum_base.shape, F32),
        ),
        in_specs=[VMEM] * (2 + 2 * count + len(pieces)),
        out_specs=[HBM if final else VMEM] * 2,
        scratch_shapes=scratch,
        compiler_params=params_of(),
        name="contract",
    )(base, momentum_base, *[one[0] for one in blocks], *[one[2] for one in blocks], *[one[1] for one in pieces])


def per_device(section_inputs, cotangent, crop_rows, drift, params, momentum):
    sections = lax.axis_size("section")
    here, replicas = lax.axis_index("replica"), lax.axis_size("replica")
    micro, rows, cols, width = section_inputs.shape[2:]
    length = rows * cols
    share = width // replicas
    taps = params.shape[1]
    scale = (9.0 * width) ** (-0.5)
    bits = [1 << n for n in reversed(range((replicas - 1).bit_length()))]
    x = section_inputs.reshape(micro, length, width)
    cot = cotangent.reshape(micro, length, width)

    def swap(value, bit):
        return lax.ppermute(value, "replica", [(i, i ^ bit) for i in range(replicas)])

    def spread_out(value, through):
        held = [(0, value)]
        for bit in through:
            held += [(at | bit, swap(one, bit)) for at, one in held]
        return held

    def hop(value, step):
        return lax.ppermute(value, "section", [(sections - 1 - step, sections - 2 - step)])

    def slice_of(value, relative):
        at = jnp.bitwise_xor(here, relative) * share
        return lax.dynamic_slice_in_dim(value, at, share, 1).astype(F32)

    low, last = bits[1:], bits[0]
    own, near = momentum[0], drift[0, 0]
    far = swap(near, 1) if low else jnp.zeros_like(near)
    weights, x_near, slopes, tops = prepare(crop_rows, x, cot, params[0], rows, cols)
    arrived = [[top] for top in tops]
    for step in range(sections - 1):
        leaving = [stage(arrived[m], slopes[m], weights, rows, cols) for m in range(micro)]
        for m in range(micro):
            arrived[m].append(hop(leaving[m], step))
        if step == 0:
            far, x_sent = after(far, *leaving), after(x_near, *leaving)
            if len(low) < 2:
                ours, rest = outgoing(near, far, own, last, replicas)
            else:
                live = {j: slice_of(near, j) + slice_of(far, j) for j in range(0, replicas, 2)}
                for bit in reversed(low[:-1]):
                    got = {j: swap(v.astype(BF16), bit) for j, v in live.items() if j & bit}
                    live = {j: v + got[j | bit].astype(F32) for j, v in live.items() if not j & bit}
                ours = jnp.concatenate([1.33 / replicas * live[0] + 0.567 * own, live[last]], axis=1).astype(BF16)
                rest = 0.9 * own + live[0] / replicas
        arrived[0][-1] = after(arrived[0][-1], *leaving[1:], *([ours] if step == 0 else []))
    pair, momentum_base = incoming(ours, swap(ours, last), rest, replicas)
    pieces = spread_out(pair, low)
    base = params[0]

    turned = {at: turned_taps(one, rows, cols) for at, one in spread_out(x_sent, bits)}

    gain = 0.5 * scale / replicas
    gains = (-1.33 * gain, gain)
    blocks = []
    arrived[0][-1] = after(arrived[0][-1], *turned.values())
    for m in range(micro):
        local = (sum(one.astype(F32) for one in arrived[m]) * slopes[m]).astype(BF16)
        if m < micro - 1:
            blocks += [(turned[at], m, one) for at, one in spread_out(local, bits)]
            continue
        for at, one in spread_out(local, low):
            blocks.append((turned[at], m, one))
        for at in range(0, len(blocks), 6):
            base, momentum_base = contract(base, momentum_base, blocks[at : at + 6], gains, False, pieces, last)
            pieces = ()
        crossed = after(swap(local, last), base)
        blocks = [(turned[at | last], m, one) for at, one in spread_out(crossed, low)]
    for at in range(0, len(blocks), 2):
        base, momentum_base = contract(base, momentum_base, blocks[at : at + 2], gains, at + 2 >= len(blocks))
    return (base[None], momentum_base[None])


def solution(mesh):
    placed = (
        P(("groups", "replica"), "section", None, None, None, None),
        P(("groups", "replica"), None, None, None, None),
        P(("groups", "replica"), None),
        P(("groups", "replica"), "section", None, None, None),
        P(("groups", "section"), None, None, None),
        P(("groups", "section"), None, "replica", None),
    )
    return jax.shard_map(
        per_device,
        mesh=mesh,
        in_specs=placed,
        out_specs=(
            P(("groups", "section"), None, None, None),
            P(("groups", "section"), None, "replica", None),
        ),
        check_vma=False,
    )
```

```python
import functools
import math

import jax
import jax.numpy as jnp
import numpy as np
from jax import lax
from jax.experimental import pallas as pl
from jax.experimental.pallas import tpu as pltpu
from jax.sharding import PartitionSpec as P

LATS = 721
MIDDLE = (LATS - 1) / 2.0
NORM = float(np.mean(np.cos(math.pi * (np.arange(LATS) - MIDDLE) / (LATS - 1))))
F32 = jnp.float32
BF16 = jnp.bfloat16
NN = (((1,), (0,)), ((), ()))
NT = (((1,), (1,)), ((), ()))
VMEM_LIMIT = 30 << 20
STAGE_WEIGHT = 6
CONTRACT_COST = 300_000_000
VMEM = pl.BlockSpec(memory_space=pltpu.VMEM)
HBM = pl.BlockSpec(memory_space=pltpu.HBM)


def params_of(**more):
    return pltpu.CompilerParams(vmem_limit_bytes=VMEM_LIMIT, **more)


def spread(ref, at, values, rows, cols):
    length = rows * cols
    column = lax.broadcasted_iota(jnp.int32, values.shape, 0) % cols
    zeros = jnp.zeros((cols, values.shape[1]), BF16)
    for b in range(3):
        if b == 0:
            moved = jnp.where(column == 0, 0.0, pltpu.roll(values, 1, 0))
        elif b == 2:
            moved = jnp.where(column == cols - 1, 0.0, pltpu.roll(values, length - 1, 0))
        else:
            moved = values
        ref[(*at, b, pl.ds(0, cols), slice(None))] = zeros
        ref[(*at, b, pl.ds(cols, length), slice(None))] = moved.astype(BF16)
        ref[(*at, b, pl.ds(cols + length, cols), slice(None))] = zeros


def stay(value):
    return pltpu.with_memory_space_constraint(value, pltpu.HBM)


def after(value, *others):
    return lax.optimization_barrier((value, *others))[0]


def product_cost(count, length, width, moved):
    return pl.CostEstimate(flops=2 * count * length * width * width, bytes_accessed=moved, transcendentals=0)


def gradient_in(grad, local, shifted, w_ref, rows, cols):
    length, width = grad.shape
    spread(shifted, (), local, rows, cols)
    total = None
    for a in range(3):
        for b in range(3):
            at = (2 - a) * cols
            term = lax.dot_general(
                shifted[2 - b, at : at + length, :], w_ref[3 * a + b], NT, preferred_element_type=F32
            )
            total = term if total is None else total + term
    return grad + (9.0 * width) ** (-0.5) * total


def prepare(crop_rows, inputs, cotangent, weights, rows, cols):
    micro, length, width = inputs.shape
    taps = weights.shape[0]
    scale = (9.0 * width) ** (-0.5)

    def kernel(crop_ref, x_ref, cot_ref, w_ref, wbf_ref, x_now, *refs):
        slopes, tops, refs = refs[:micro], refs[micro : 2 * micro], refs[2 * micro :]
        cot_now, crop_now, shifted, w_now, sems = refs
        load_x = pltpu.make_async_copy(x_ref, x_now, sems.at[0])
        load_cot = pltpu.make_async_copy(cot_ref, cot_now, sems.at[1])
        load_crop = pltpu.make_async_copy(crop_ref, crop_now, sems.at[2])
        loads = [pltpu.make_async_copy(w_ref.at[k], w_now.at[k], sems.at[3 + k]) for k in range(taps)]
        for load in (load_crop, load_x, *loads, load_cot):
            load.start()
        load_crop.wait()
        is_last = lax.axis_index("section") == lax.axis_size("section") - 1
        factors = []
        for m in range(micro):
            here = lax.broadcasted_iota(jnp.int32, (rows, 128), 0) + crop_now[0, m]
            factor = jnp.cos(math.pi * (here.astype(F32) - MIDDLE) / (LATS - 1)) / NORM
            factors.append(jnp.where(is_last, factor, 0.0))
        load_x.wait()
        for m in range(micro):
            spread(shifted, (m,), x_now[m].astype(F32), rows, cols)

        def product(m, k, total):
            a, b = divmod(k, 3)
            term = lax.dot_general(
                shifted[m, b, a * cols : a * cols + length, :], wbf_ref[k], NN, preferred_element_type=F32
            )
            return term if total is None else total + term

        total = None
        for k in range(taps):
            loads[k].wait()
            wbf_ref[k] = w_now[k].astype(BF16)
            total = product(0, k, total)
        for m in range(micro):
            if m:
                total = None
                for k in range(taps):
                    total = product(m, k, total)
            else:
                load_cot.wait()
            tangent = jnp.tanh(total * scale)
            slopes[m][...] = 1.0 - tangent * tangent
            for i in range(rows):
                line = jnp.broadcast_to(factors[m][i : i + 1], (cols, 128))
                line = jnp.concatenate([line] * (width // 128), axis=1)
                at = slice(i * cols, (i + 1) * cols)
                tops[m][at, :] = (cot_now[m, at, :].astype(F32) * line).astype(BF16)

    shapes = [jax.ShapeDtypeStruct(weights.shape, BF16), jax.ShapeDtypeStruct(inputs.shape, BF16)]
    shapes += [jax.ShapeDtypeStruct((length, width), F32)] * micro
    shapes += [jax.ShapeDtypeStruct((length, width), BF16)] * micro
    out = pl.pallas_call(
        kernel,
        out_shape=shapes,
        in_specs=[HBM] * 4,
        out_specs=[VMEM] * len(shapes),
        scratch_shapes=[
            pltpu.VMEM(inputs.shape, BF16),
            pltpu.SMEM(crop_rows.shape, jnp.int32),
            pltpu.VMEM((micro, 3, length + 2 * cols, width), BF16),
            pltpu.VMEM(weights.shape, F32),
            pltpu.SemaphoreType.DMA((3 + taps,)),
        ],
        compiler_params=params_of(),
        name="prepare",
    )(*[stay(one) for one in (crop_rows, inputs, cotangent, weights)])
    return out[0], out[1], out[2 : 2 + micro], out[2 + micro :]


def stage(step, arrived, slope, weights, rows, cols):
    taps, width, _ = weights.shape
    length = rows * cols
    count = len(arrived)

    def kernel(*refs):
        parts, (slope_ref, w_ref, out_ref, shifted) = refs[:count], refs[count:]

        @pl.when(lax.axis_index("section") == lax.axis_size("section") - 1 - step)
        def _():
            grad = parts[0][...].astype(F32)
            for part in parts[1:]:
                grad += part[...].astype(F32)
            local = (grad * slope_ref[...]).astype(BF16).astype(F32)
            out_ref[...] = gradient_in(grad, local, shifted, w_ref, rows, cols).astype(BF16)

    return pl.pallas_call(
        kernel,
        out_shape=jax.ShapeDtypeStruct((length, width), BF16),
        in_specs=[VMEM] * (count + 2),
        out_specs=VMEM,
        scratch_shapes=[pltpu.VMEM((3, length + 2 * cols, width), BF16)],
        compiler_params=params_of(),
        cost_estimate=product_cost(STAGE_WEIGHT * taps, length, width, 2 * weights.size),
        name="stage",
    )(*arrived, slope, weights)


def turned_taps(inputs, rows, cols):
    blocks, length, width = inputs.shape

    def kernel(x_ref, out_ref, shifted):
        for n in range(blocks):
            spread(shifted, (), x_ref[n].astype(F32), rows, cols)
            for a in range(3):
                for b in range(3):
                    out_ref[n, 3 * a + b] = shifted[b, a * cols : a * cols + length, :].T

    return pl.pallas_call(
        kernel,
        out_shape=jax.ShapeDtypeStruct((blocks, 9, width, length), BF16),
        in_specs=[VMEM],
        out_specs=VMEM,
        scratch_shapes=[pltpu.VMEM((3, length + 2 * cols, width), BF16)],
        compiler_params=params_of(),
        name="turned_taps",
    )(inputs)


def outgoing(near, far, momentum, last, replicas):
    taps, width, _ = near.shape
    share = momentum.shape[1]

    def kernel(near_ref, far_ref, own_ref, out_ref, rest_ref, total):
        here = lax.axis_index("replica")
        own_rows = pl.ds(pl.multiple_of(here * share, share), share)
        other_rows = pl.ds(pl.multiple_of(jnp.bitwise_xor(here, last) * share, share), share)
        for k in range(taps):
            total[k % 2] = near_ref[k].astype(F32) + far_ref[k].astype(F32)
            mine = total[k % 2, own_rows, :]
            out_ref[k, :share] = (1.33 / replicas * mine + 0.567 * own_ref[k]).astype(BF16)
            out_ref[k, share:] = total[k % 2, other_rows, :].astype(BF16)
            rest_ref[k] = 0.9 * own_ref[k] + mine / replicas

    return pl.pallas_call(
        kernel,
        out_shape=(
            jax.ShapeDtypeStruct((taps, 2 * share, width), BF16),
            jax.ShapeDtypeStruct(momentum.shape, F32),
        ),
        in_specs=[VMEM] * 3,
        out_specs=[VMEM] * 2,
        scratch_shapes=[pltpu.VMEM((2, width, width), F32)],
        compiler_params=params_of(),
        name="outgoing",
    )(near, far, momentum)


def incoming(ours, theirs, rest, replicas):
    share = rest.shape[1]

    def kernel(ours_ref, theirs_ref, rest_ref, out_ref, momentum_ref):
        for k in range(rest.shape[0]):
            mine, there = ours_ref[k].astype(F32), theirs_ref[k].astype(F32)
            out_ref[k, :share] = (mine[:share] + 1.33 / replicas * there[share:]).astype(BF16)
            out_ref[k, share:] = (there[:share] + 1.33 / replicas * mine[share:]).astype(BF16)
            momentum_ref[k] = rest_ref[k] + there[share:] / replicas

    return pl.pallas_call(
        kernel,
        out_shape=(jax.ShapeDtypeStruct(ours.shape, BF16), jax.ShapeDtypeStruct(rest.shape, F32)),
        in_specs=[VMEM] * 3,
        out_specs=[VMEM] * 2,
        compiler_params=params_of(),
        name="incoming",
    )(ours, theirs, rest)


def contract(base, momentum_base, blocks, gains, final, pieces=(), last=0, cost=0):
    taps, width, _ = base.shape
    share = momentum_base.shape[1]
    count = len(blocks)

    def kernel(base_ref, mom_ref, *refs):
        turned, local, refs = refs[:count], refs[count : 2 * count], refs[2 * count :]
        taken, refs = refs[: len(pieces)], refs[len(pieces) :]
        out_ref, mom_out_ref, total = refs[:3]
        if final:
            out_now, mom_now, sems = refs[3:]
        else:
            out_now, mom_now = out_ref, mom_out_ref
        here = lax.axis_index("replica")
        own = pl.multiple_of(here * share, share)
        copies = []
        for k in range(taps):
            acc = None
            for n in range(count):
                term = lax.dot_general(turned[n][blocks[n][1], k], local[n][...], NN, preferred_element_type=F32)
                acc = term if acc is None else acc + term
            total[k % 2] = acc
            out_now[k] = base_ref[k] + gains[0] * acc
            for (at, low_tap, _), piece in zip(pieces, taken):
                j = k - low_tap
                for n in range(2 if 0 <= j < piece.shape[0] else 0):
                    where = jnp.bitwise_xor(here, at | n * last) * share
                    lines = pl.ds(pl.multiple_of(where, share), share)
                    out_now[k, lines, :] -= piece[j, n * share : (n + 1) * share].astype(F32)
            mom_now[k] = mom_ref[k] + gains[1] * total[k % 2, pl.ds(own, share), :]
            if final:
                copies.append(pltpu.make_async_copy(out_now.at[k], out_ref.at[k], sems.at[0, k]))
                copies.append(pltpu.make_async_copy(mom_now.at[k], mom_out_ref.at[k], sems.at[1, k]))
                copies[-2].start()
                copies[-1].start()
        for copy in copies:
            copy.wait()

    scratch = [pltpu.VMEM((2, width, width), F32)]
    if final:
        scratch += [
            pltpu.VMEM(base.shape, F32),
            pltpu.VMEM(momentum_base.shape, F32),
            pltpu.SemaphoreType.DMA((2, taps)),
        ]
    return pl.pallas_call(
        kernel,
        out_shape=(
            jax.ShapeDtypeStruct(base.shape, F32),
            jax.ShapeDtypeStruct(momentum_base.shape, F32),
        ),
        in_specs=[VMEM] * (2 + 2 * count + len(pieces)),
        out_specs=[HBM if final else VMEM] * 2,
        scratch_shapes=scratch,
        compiler_params=params_of(),
        cost_estimate=pl.CostEstimate(flops=cost, bytes_accessed=0, transcendentals=0),
        name="contract",
    )(base, momentum_base, *[one[0] for one in blocks], *[one[2] for one in blocks], *[one[2] for one in pieces])


def per_device(section_inputs, cotangent, crop_rows, drift, params, momentum):
    sections = lax.axis_size("section")
    here, replicas = lax.axis_index("replica"), lax.axis_size("replica")
    micro, rows, cols, width = section_inputs.shape[2:]
    length = rows * cols
    share = width // replicas
    taps = params.shape[1]
    scale = (9.0 * width) ** (-0.5)
    bits = [1 << n for n in reversed(range((replicas - 1).bit_length()))]
    x = section_inputs.reshape(micro, length, width)
    cot = cotangent.reshape(micro, length, width)

    def swap(value, bit):
        return lax.ppermute(value, "replica", [(i, i ^ bit) for i in range(replicas)])

    def spread_out(value, through):
        held = [(0, value)]
        for bit in through:
            held += [(at | bit, swap(one, bit)) for at, one in held]
        return held

    def hop(value, step):
        return lax.ppermute(value, "section", [(sections - 1 - step, sections - 2 - step)])

    def slice_of(value, relative):
        at = jnp.bitwise_xor(here, relative) * share
        return lax.dynamic_slice_in_dim(value, at, share, 1).astype(F32)

    low, last = bits[1:], bits[0]
    own, near = momentum[0], drift[0, 0]
    far = swap(near, 1) if low else jnp.zeros_like(near)
    weights, x_near, slopes, tops = prepare(crop_rows, x, cot, params[0], rows, cols)
    arrived = [[top] for top in tops]
    for step in range(sections - 1):
        leaving = [stage(step, arrived[m], slopes[m], weights, rows, cols) for m in range(micro)]
        for m in range(micro):
            arrived[m].append(hop(leaving[m], step))
        if step == 0:
            far, x_sent = after(far, *leaving), after(x_near, *leaving)
            if len(low) < 2:
                ours, rest = outgoing(near, far, own, last, replicas)
            else:
                live = {j: slice_of(near, j) + slice_of(far, j) for j in range(0, replicas, 2)}
                for bit in reversed(low[:-1]):
                    got = {j: swap(v.astype(BF16), bit) for j, v in live.items() if j & bit}
                    live = {j: v + got[j | bit].astype(F32) for j, v in live.items() if not j & bit}
                ours = jnp.concatenate([1.33 / replicas * live[0] + 0.567 * own, live[last]], axis=1).astype(BF16)
                rest = 0.9 * own + live[0] / replicas
        arrived[0][-1] = after(arrived[0][-1], *leaving[1:], *([ours] if step == 0 else []))
    theirs = swap(ours, last)

    turned = {at: turned_taps(one, rows, cols) for at, one in spread_out(x_sent, bits)}

    gain = 0.5 * scale / replicas
    gains = (-1.33 * gain, gain)
    arrived[0][-1] = after(arrived[0][-1], *turned.values())
    near, crossed = [], []
    for m in range(micro):
        local = (sum(one.astype(F32) for one in arrived[m]) * slopes[m]).astype(BF16)
        crossed.append(swap(local, last))
        near.append([(turned[at], m, one) for at, one in spread_out(local, low)])
    base, momentum_base = params[0], rest
    for m in range(micro):
        if m:
            at, _, one = near[m][-1]
            near[m][-1] = (at, m, after(one, base))
        else:
            base = after(base, crossed[0])
        base, momentum_base = contract(base, momentum_base, near[m], gains, False, cost=CONTRACT_COST)
        if m == 0:
            pair, momentum_base = incoming(ours, after(theirs, base), momentum_base, replicas)
    blocks = []
    for m in range(micro):
        blocks += [(turned[at | last], m, one) for at, one in spread_out(after(crossed[m], base), low)]
    pieces = []
    for k in range(0, taps, 3):
        pieces += [(at, k, one) for at, one in spread_out(pair[k : k + 3], low)]
    for at in range(0, len(blocks), 4):
        base, momentum_base = contract(
            base, momentum_base, blocks[at : at + 4], gains, at + 4 >= len(blocks), pieces, last
        )
        pieces = ()
    return (base[None], momentum_base[None])


def solution(mesh):
    placed = (
        P(("groups", "replica"), "section", None, None, None, None),
        P(("groups", "replica"), None, None, None, None),
        P(("groups", "replica"), None),
        P(("groups", "replica"), "section", None, None, None),
        P(("groups", "section"), None, None, None),
        P(("groups", "section"), None, "replica", None),
    )
    return jax.shard_map(
        per_device,
        mesh=mesh,
        in_specs=placed,
        out_specs=(
            P(("groups", "section"), None, None, None),
            P(("groups", "section"), None, "replica", None),
        ),
        check_vma=False,
    )
```

```python
import functools
import math

import jax
import jax.numpy as jnp
import numpy as np
from jax import lax
from jax.experimental import pallas as pl
from jax.experimental.pallas import tpu as pltpu
from jax.sharding import PartitionSpec as P

LATS = 721
MIDDLE = (LATS - 1) / 2.0
NORM = float(np.mean(np.cos(math.pi * (np.arange(LATS) - MIDDLE) / (LATS - 1))))
F32 = jnp.float32
BF16 = jnp.bfloat16
NN = (((1,), (0,)), ((), ()))
NT = (((1,), (1,)), ((), ()))
VMEM_LIMIT = 30 << 20
FIRST_WEIGHT = 0
STAGE_WEIGHT = 6
LATER_WEIGHT = 1
CONTRACT_COST = 300_000_000
VMEM = pl.BlockSpec(memory_space=pltpu.VMEM)
HBM = pl.BlockSpec(memory_space=pltpu.HBM)


def params_of(**more):
    return pltpu.CompilerParams(vmem_limit_bytes=VMEM_LIMIT, **more)


def spread(ref, at, values, rows, cols):
    length = rows * cols
    column = lax.broadcasted_iota(jnp.int32, values.shape, 0) % cols
    zeros = jnp.zeros((cols, values.shape[1]), BF16)
    for b in range(3):
        if b == 0:
            moved = jnp.where(column == 0, 0.0, pltpu.roll(values, 1, 0))
        elif b == 2:
            moved = jnp.where(column == cols - 1, 0.0, pltpu.roll(values, length - 1, 0))
        else:
            moved = values
        ref[(*at, b, pl.ds(0, cols), slice(None))] = zeros
        ref[(*at, b, pl.ds(cols, length), slice(None))] = moved.astype(BF16)
        ref[(*at, b, pl.ds(cols + length, cols), slice(None))] = zeros


def stay(value):
    return pltpu.with_memory_space_constraint(value, pltpu.HBM)


def after(value, *others):
    return lax.optimization_barrier((value, *others))[0]


def product_cost(count, length, width, moved):
    return pl.CostEstimate(flops=2 * count * length * width * width, bytes_accessed=moved, transcendentals=0)


def gradient_in(grad, local, shifted, w_ref, rows, cols):
    length, width = grad.shape
    spread(shifted, (), local, rows, cols)
    total = None
    for a in range(3):
        for b in range(3):
            at = (2 - a) * cols
            term = lax.dot_general(
                shifted[2 - b, at : at + length, :], w_ref[3 * a + b], NT, preferred_element_type=F32
            )
            total = term if total is None else total + term
    return grad + (9.0 * width) ** (-0.5) * total


def prepare(crop_rows, inputs, cotangent, weights, rows, cols):
    micro, length, width = inputs.shape
    taps = weights.shape[0]
    scale = (9.0 * width) ** (-0.5)

    def kernel(crop_ref, x_ref, cot_ref, w_ref, wbf_ref, x_now, *refs):
        slopes, tops, refs = refs[:micro], refs[micro : 2 * micro], refs[2 * micro :]
        cot_now, crop_now, shifted, w_now, sems = refs
        load_x = pltpu.make_async_copy(x_ref, x_now, sems.at[0])
        load_cot = pltpu.make_async_copy(cot_ref, cot_now, sems.at[1])
        load_crop = pltpu.make_async_copy(crop_ref, crop_now, sems.at[2])
        loads = [pltpu.make_async_copy(w_ref.at[k], w_now.at[k], sems.at[3 + k]) for k in range(taps)]
        for load in (load_crop, load_x, *loads, load_cot):
            load.start()
        load_crop.wait()
        is_last = lax.axis_index("section") == lax.axis_size("section") - 1
        factors = []
        for m in range(micro):
            here = lax.broadcasted_iota(jnp.int32, (rows, 128), 0) + crop_now[0, m]
            factor = jnp.cos(math.pi * (here.astype(F32) - MIDDLE) / (LATS - 1)) / NORM
            factors.append(jnp.where(is_last, factor, 0.0))
        load_x.wait()
        for m in range(micro):
            spread(shifted, (m,), x_now[m].astype(F32), rows, cols)

        def product(m, k, total):
            a, b = divmod(k, 3)
            term = lax.dot_general(
                shifted[m, b, a * cols : a * cols + length, :], wbf_ref[k], NN, preferred_element_type=F32
            )
            return term if total is None else total + term

        total = None
        for k in range(taps):
            loads[k].wait()
            wbf_ref[k] = w_now[k].astype(BF16)
            total = product(0, k, total)
        for m in range(micro):
            if m:
                total = None
                for k in range(taps):
                    total = product(m, k, total)
            else:
                load_cot.wait()
            tangent = jnp.tanh(total * scale)
            slopes[m][...] = 1.0 - tangent * tangent
            for i in range(rows):
                line = jnp.broadcast_to(factors[m][i : i + 1], (cols, 128))
                line = jnp.concatenate([line] * (width // 128), axis=1)
                at = slice(i * cols, (i + 1) * cols)
                tops[m][at, :] = (cot_now[m, at, :].astype(F32) * line).astype(BF16)

    shapes = [jax.ShapeDtypeStruct(weights.shape, BF16), jax.ShapeDtypeStruct(inputs.shape, BF16)]
    shapes += [jax.ShapeDtypeStruct((length, width), F32)] * micro
    shapes += [jax.ShapeDtypeStruct((length, width), BF16)] * micro
    out = pl.pallas_call(
        kernel,
        out_shape=shapes,
        in_specs=[HBM] * 4,
        out_specs=[VMEM] * len(shapes),
        scratch_shapes=[
            pltpu.VMEM(inputs.shape, BF16),
            pltpu.SMEM(crop_rows.shape, jnp.int32),
            pltpu.VMEM((micro, 3, length + 2 * cols, width), BF16),
            pltpu.VMEM(weights.shape, F32),
            pltpu.SemaphoreType.DMA((3 + taps,)),
        ],
        compiler_params=params_of(),
        name="prepare",
    )(*[stay(one) for one in (crop_rows, inputs, cotangent, weights)])
    return out[0], out[1], out[2 : 2 + micro], out[2 + micro :]


def stage(step, arrived, slope, weights, rows, cols, weight):
    taps, width, _ = weights.shape
    length = rows * cols
    count = len(arrived)

    def kernel(*refs):
        parts, (slope_ref, w_ref, out_ref, shifted) = refs[:count], refs[count:]

        @pl.when(lax.axis_index("section") == lax.axis_size("section") - 1 - step)
        def _():
            grad = parts[0][...].astype(F32)
            for part in parts[1:]:
                grad += part[...].astype(F32)
            local = (grad * slope_ref[...]).astype(BF16).astype(F32)
            out_ref[...] = gradient_in(grad, local, shifted, w_ref, rows, cols).astype(BF16)

    return pl.pallas_call(
        kernel,
        out_shape=jax.ShapeDtypeStruct((length, width), BF16),
        in_specs=[VMEM] * (count + 2),
        out_specs=VMEM,
        scratch_shapes=[pltpu.VMEM((3, length + 2 * cols, width), BF16)],
        compiler_params=params_of(),
        cost_estimate=product_cost(weight * taps, length, width, 2 * weights.size),
        name="stage",
    )(*arrived, slope, weights)


def turned_taps(inputs, rows, cols):
    blocks, length, width = inputs.shape

    def kernel(x_ref, out_ref, shifted):
        for n in range(blocks):
            spread(shifted, (), x_ref[n].astype(F32), rows, cols)
            for a in range(3):
                for b in range(3):
                    out_ref[n, 3 * a + b] = shifted[b, a * cols : a * cols + length, :].T

    return pl.pallas_call(
        kernel,
        out_shape=jax.ShapeDtypeStruct((blocks, 9, width, length), BF16),
        in_specs=[VMEM],
        out_specs=VMEM,
        scratch_shapes=[pltpu.VMEM((3, length + 2 * cols, width), BF16)],
        compiler_params=params_of(),
        name="turned_taps",
    )(inputs)


def outgoing(inputs, near, far, momentum, last, replicas):
    taps, width, _ = near.shape
    share = momentum.shape[1]
    head = inputs.shape[0] * inputs.shape[1]

    def kernel(x_ref, near_ref, far_ref, own_ref, out_ref, rest_ref, total):
        for m in range(inputs.shape[0]):
            out_ref[m * inputs.shape[1] : (m + 1) * inputs.shape[1]] = x_ref[m]
        here = lax.axis_index("replica")
        own_rows = pl.ds(pl.multiple_of(here * share, share), share)
        other_rows = pl.ds(pl.multiple_of(jnp.bitwise_xor(here, last) * share, share), share)
        for k in range(taps):
            total[k % 2] = near_ref[k].astype(F32) + far_ref[k].astype(F32)
            mine = total[k % 2, own_rows, :]
            at = head + k * 2 * share
            out_ref[at : at + share] = (1.33 / replicas * mine + 0.567 * own_ref[k]).astype(BF16)
            out_ref[at + share : at + 2 * share] = total[k % 2, other_rows, :].astype(BF16)
            rest_ref[k] = 0.9 * own_ref[k] + mine / replicas

    return pl.pallas_call(
        kernel,
        out_shape=(
            jax.ShapeDtypeStruct((head + taps * 2 * share, width), BF16),
            jax.ShapeDtypeStruct(momentum.shape, F32),
        ),
        in_specs=[VMEM] * 4,
        out_specs=[VMEM] * 2,
        scratch_shapes=[pltpu.VMEM((2, width, width), F32)],
        compiler_params=params_of(),
        name="outgoing",
    )(inputs, near, far, momentum)


def incoming(ours, theirs, rest, replicas):
    taps, share, width = rest.shape
    head = ours.shape[0] - taps * 2 * share

    def kernel(ours_ref, theirs_ref, rest_ref, out_ref, momentum_ref):
        for k in range(taps):
            lines = slice(head + k * 2 * share, head + (k + 1) * 2 * share)
            mine, there = ours_ref[lines].astype(F32), theirs_ref[lines].astype(F32)
            out_ref[k, :share] = (mine[:share] + 1.33 / replicas * there[share:]).astype(BF16)
            out_ref[k, share:] = (there[:share] + 1.33 / replicas * mine[share:]).astype(BF16)
            momentum_ref[k] = rest_ref[k] + there[share:] / replicas

    return pl.pallas_call(
        kernel,
        out_shape=(jax.ShapeDtypeStruct((taps, 2 * share, width), BF16), jax.ShapeDtypeStruct(rest.shape, F32)),
        in_specs=[VMEM] * 3,
        out_specs=[VMEM] * 2,
        compiler_params=params_of(),
        name="incoming",
    )(ours, theirs, rest)


def contract(base, momentum_base, blocks, gains, final, pieces=(), last=0, cost=0):
    taps, width, _ = base.shape
    share = momentum_base.shape[1]
    count = len(blocks)

    def kernel(base_ref, mom_ref, *refs):
        turned, local, refs = refs[:count], refs[count : 2 * count], refs[2 * count :]
        taken, refs = refs[: len(pieces)], refs[len(pieces) :]
        out_ref, mom_out_ref, total = refs[:3]
        if final:
            out_now, mom_now, sems = refs[3:]
        else:
            out_now, mom_now = out_ref, mom_out_ref
        here = lax.axis_index("replica")
        own = pl.multiple_of(here * share, share)
        copies = []
        for k in range(taps):
            acc = None
            for n in range(count):
                term = lax.dot_general(turned[n][blocks[n][1], k], local[n][...], NN, preferred_element_type=F32)
                acc = term if acc is None else acc + term
            total[k % 2] = acc
            out_now[k] = base_ref[k] + gains[0] * acc
            for (at, low_tap, _), piece in zip(pieces, taken):
                j = k - low_tap
                for n in range(2 if 0 <= j < piece.shape[0] else 0):
                    where = jnp.bitwise_xor(here, at | n * last) * share
                    lines = pl.ds(pl.multiple_of(where, share), share)
                    out_now[k, lines, :] -= piece[j, n * share : (n + 1) * share].astype(F32)
            mom_now[k] = mom_ref[k] + gains[1] * total[k % 2, pl.ds(own, share), :]
            if final:
                copies.append(pltpu.make_async_copy(out_now.at[k], out_ref.at[k], sems.at[0, k]))
                copies.append(pltpu.make_async_copy(mom_now.at[k], mom_out_ref.at[k], sems.at[1, k]))
                copies[-2].start()
                copies[-1].start()
        for copy in copies:
            copy.wait()

    scratch = [pltpu.VMEM((2, width, width), F32)]
    if final:
        scratch += [
            pltpu.VMEM(base.shape, F32),
            pltpu.VMEM(momentum_base.shape, F32),
            pltpu.SemaphoreType.DMA((2, taps)),
        ]
    return pl.pallas_call(
        kernel,
        out_shape=(
            jax.ShapeDtypeStruct(base.shape, F32),
            jax.ShapeDtypeStruct(momentum_base.shape, F32),
        ),
        in_specs=[VMEM] * (2 + 2 * count + len(pieces)),
        out_specs=[HBM if final else VMEM] * 2,
        scratch_shapes=scratch,
        compiler_params=params_of(),
        cost_estimate=pl.CostEstimate(flops=cost, bytes_accessed=0, transcendentals=0),
        name="contract",
    )(base, momentum_base, *[one[0] for one in blocks], *[one[2] for one in blocks], *[one[2] for one in pieces])


def per_device(section_inputs, cotangent, crop_rows, drift, params, momentum):
    sections = lax.axis_size("section")
    here, replicas = lax.axis_index("replica"), lax.axis_size("replica")
    micro, rows, cols, width = section_inputs.shape[2:]
    length = rows * cols
    share = width // replicas
    taps = params.shape[1]
    scale = (9.0 * width) ** (-0.5)
    bits = [1 << n for n in reversed(range((replicas - 1).bit_length()))]
    x = section_inputs.reshape(micro, length, width)
    cot = cotangent.reshape(micro, length, width)

    def swap(value, bit):
        return lax.ppermute(value, "replica", [(i, i ^ bit) for i in range(replicas)])

    def spread_out(value, through):
        held = [(0, value)]
        for bit in through:
            held += [(at | bit, swap(one, bit)) for at, one in held]
        return held

    def hop(value, step):
        return lax.ppermute(value, "section", [(sections - 1 - step, sections - 2 - step)])

    def slice_of(value, relative):
        at = jnp.bitwise_xor(here, relative) * share
        return lax.dynamic_slice_in_dim(value, at, share, 1).astype(F32)

    low, last = bits[1:], bits[0]
    own, near = momentum[0], drift[0, 0]
    far = swap(near, 1) if low else jnp.zeros_like(near)
    weights, x_near, slopes, tops = prepare(crop_rows, x, cot, params[0], rows, cols)
    arrived = [[top] for top in tops]
    for step in range(sections - 1):
        hints = [LATER_WEIGHT if step else STAGE_WEIGHT] * micro
        hints[0] = hints[0] if step else FIRST_WEIGHT
        leaving = [stage(step, arrived[m], slopes[m], weights, rows, cols, hints[m]) for m in range(micro)]
        for m in range(micro):
            arrived[m].append(hop(leaving[m], step))
        if step == 0:
            far, x_sent = after(far, *leaving), after(x_near, *leaving)
            if len(low) < 2:
                ours, rest = outgoing(x_sent, near, far, own, last, replicas)
            else:
                live = {j: slice_of(near, j) + slice_of(far, j) for j in range(0, replicas, 2)}
                for bit in reversed(low[:-1]):
                    got = {j: swap(v.astype(BF16), bit) for j, v in live.items() if j & bit}
                    live = {j: v + got[j | bit].astype(F32) for j, v in live.items() if not j & bit}
                ours = jnp.concatenate([1.33 / replicas * live[0] + 0.567 * own, live[last]], axis=1).astype(BF16)
                ours = jnp.concatenate([x_sent.reshape(-1, width), ours.reshape(-1, width)])
                rest = 0.9 * own + live[0] / replicas
        arrived[0][-1] = after(arrived[0][-1], *leaving[1:], *([ours] if step == 0 else []))
    theirs = swap(ours, last)


    x_there = theirs[: micro * length].reshape(x.shape)
    x_all = spread_out(x_sent, low) + [(at | last, one) for at, one in spread_out(x_there, low)]
    turned = {at: turned_taps(one, rows, cols) for at, one in x_all}

    gain = 0.5 * scale / replicas
    gains = (-1.33 * gain, gain)
    arrived[0][-1] = after(arrived[0][-1], *[one for at, one in turned.items() if at < last])
    near, crossed = [], []
    for m in range(micro):
        local = (sum(one.astype(F32) for one in arrived[m]) * slopes[m]).astype(BF16)
        crossed.append(swap(local, last))
        near.append([(turned[at], m, one) for at, one in spread_out(local, low)])
    base, momentum_base = params[0], rest
    for m in range(micro):
        if m:
            at, _, one = near[m][-1]
            near[m][-1] = (at, m, after(one, base))
        else:
            base = after(base, crossed[0])
        base, momentum_base = contract(base, momentum_base, near[m], gains, False, cost=CONTRACT_COST)
        if m == 0:
            pair, momentum_base = incoming(ours, theirs, momentum_base, replicas)
    blocks = []
    for m in range(micro):
        blocks += [(turned[at | last], m, one) for at, one in spread_out(after(crossed[m], base), low)]
    pieces = []
    for k in range(0, taps, 3):
        pieces += [(at, k, one) for at, one in spread_out(pair[k : k + 3], low)]
    for at in range(0, len(blocks), 4):
        base, momentum_base = contract(
            base, momentum_base, blocks[at : at + 4], gains, at + 4 >= len(blocks), pieces, last
        )
        pieces = ()
    return (base[None], momentum_base[None])


def solution(mesh):
    placed = (
        P(("groups", "replica"), "section", None, None, None, None),
        P(("groups", "replica"), None, None, None, None),
        P(("groups", "replica"), None),
        P(("groups", "replica"), "section", None, None, None),
        P(("groups", "section"), None, None, None),
        P(("groups", "section"), None, "replica", None),
    )
    return jax.shard_map(
        per_device,
        mesh=mesh,
        in_specs=placed,
        out_specs=(
            P(("groups", "section"), None, None, None),
            P(("groups", "section"), None, "replica", None),
        ),
        check_vma=False,
    )
```

```python
import functools
import math

import jax
import jax.numpy as jnp
import numpy as np
from jax import lax
from jax.experimental import pallas as pl
from jax.experimental.pallas import tpu as pltpu
from jax.sharding import PartitionSpec as P

LATS = 721
MIDDLE = (LATS - 1) / 2.0
NORM = float(np.mean(np.cos(math.pi * (np.arange(LATS) - MIDDLE) / (LATS - 1))))
F32 = jnp.float32
BF16 = jnp.bfloat16
NN = (((1,), (0,)), ((), ()))
NT = (((1,), (1,)), ((), ()))
VMEM_LIMIT = 30 << 20
FIRST_WEIGHT = 0
STAGE_WEIGHT = 6
LATER_WEIGHT = 1
CONTRACT_COST = 300_000_000
VMEM = pl.BlockSpec(memory_space=pltpu.VMEM)
HBM = pl.BlockSpec(memory_space=pltpu.HBM)


def params_of(**more):
    return pltpu.CompilerParams(vmem_limit_bytes=VMEM_LIMIT, **more)


def spread(ref, at, values, rows, cols):
    length = rows * cols
    column = lax.broadcasted_iota(jnp.int32, values.shape, 0) % cols
    zeros = jnp.zeros((cols, values.shape[1]), BF16)
    for b in range(3):
        if b == 0:
            moved = jnp.where(column == 0, 0.0, pltpu.roll(values, 1, 0))
        elif b == 2:
            moved = jnp.where(column == cols - 1, 0.0, pltpu.roll(values, length - 1, 0))
        else:
            moved = values
        ref[(*at, b, pl.ds(0, cols), slice(None))] = zeros
        ref[(*at, b, pl.ds(cols, length), slice(None))] = moved.astype(BF16)
        ref[(*at, b, pl.ds(cols + length, cols), slice(None))] = zeros


def stay(value):
    return pltpu.with_memory_space_constraint(value, pltpu.HBM)


def after(value, *others):
    return lax.optimization_barrier((value, *others))[0]


def product_cost(count, length, width, moved):
    return pl.CostEstimate(flops=2 * count * length * width * width, bytes_accessed=moved, transcendentals=0)


def gradient_in(grad, local, shifted, w_ref, rows, cols):
    length, width = grad.shape
    spread(shifted, (), local, rows, cols)
    total = None
    for a in range(3):
        for b in range(3):
            at = (2 - a) * cols
            term = lax.dot_general(
                shifted[2 - b, at : at + length, :], w_ref[3 * a + b], NT, preferred_element_type=F32
            )
            total = term if total is None else total + term
    return grad + (9.0 * width) ** (-0.5) * total


def prepare(crop_rows, inputs, cotangent, weights, rows, cols):
    micro, length, width = inputs.shape
    taps = weights.shape[0]
    scale = (9.0 * width) ** (-0.5)

    def kernel(crop_ref, x_ref, cot_ref, w_ref, wbf_ref, x_now, *refs):
        slopes, tops, refs = refs[:micro], refs[micro : 2 * micro], refs[2 * micro :]
        cot_now, crop_now, shifted, w_now, sems = refs
        load_x = pltpu.make_async_copy(x_ref, x_now, sems.at[0])
        load_cot = pltpu.make_async_copy(cot_ref, cot_now, sems.at[1])
        load_crop = pltpu.make_async_copy(crop_ref, crop_now, sems.at[2])
        loads = [pltpu.make_async_copy(w_ref.at[k], w_now.at[k], sems.at[3 + k]) for k in range(taps)]
        for load in (load_crop, load_x, *loads, load_cot):
            load.start()
        load_crop.wait()
        is_last = lax.axis_index("section") == lax.axis_size("section") - 1
        factors = []
        for m in range(micro):
            here = lax.broadcasted_iota(jnp.int32, (rows, 128), 0) + crop_now[0, m]
            factor = jnp.cos(math.pi * (here.astype(F32) - MIDDLE) / (LATS - 1)) / NORM
            factors.append(jnp.where(is_last, factor, 0.0))
        load_x.wait()
        for m in range(micro):
            spread(shifted, (m,), x_now[m].astype(F32), rows, cols)

        def product(m, k, total):
            a, b = divmod(k, 3)
            term = lax.dot_general(
                shifted[m, b, a * cols : a * cols + length, :], wbf_ref[k], NN, preferred_element_type=F32
            )
            return term if total is None else total + term

        total = None
        for k in range(taps):
            loads[k].wait()
            wbf_ref[k] = w_now[k].astype(BF16)
            total = product(0, k, total)
        for m in range(micro):
            if m:
                total = None
                for k in range(taps):
                    total = product(m, k, total)
            else:
                load_cot.wait()
            tangent = jnp.tanh(total * scale)
            slopes[m][...] = 1.0 - tangent * tangent
            for i in range(rows):
                line = jnp.broadcast_to(factors[m][i : i + 1], (cols, 128))
                line = jnp.concatenate([line] * (width // 128), axis=1)
                at = slice(i * cols, (i + 1) * cols)
                tops[m][at, :] = (cot_now[m, at, :].astype(F32) * line).astype(BF16)

    shapes = [jax.ShapeDtypeStruct(weights.shape, BF16), jax.ShapeDtypeStruct(inputs.shape, BF16)]
    shapes += [jax.ShapeDtypeStruct((length, width), F32)] * micro
    shapes += [jax.ShapeDtypeStruct((length, width), BF16)] * micro
    out = pl.pallas_call(
        kernel,
        out_shape=shapes,
        in_specs=[HBM] * 4,
        out_specs=[VMEM] * len(shapes),
        scratch_shapes=[
            pltpu.VMEM(inputs.shape, BF16),
            pltpu.SMEM(crop_rows.shape, jnp.int32),
            pltpu.VMEM((micro, 3, length + 2 * cols, width), BF16),
            pltpu.VMEM(weights.shape, F32),
            pltpu.SemaphoreType.DMA((3 + taps,)),
        ],
        compiler_params=params_of(),
        name="prepare",
    )(*[stay(one) for one in (crop_rows, inputs, cotangent, weights)])
    return out[0], out[1], out[2 : 2 + micro], out[2 + micro :]


def stage(step, arrived, slope, weights, rows, cols, weight):
    taps, width, _ = weights.shape
    length = rows * cols
    count = len(arrived)

    def kernel(*refs):
        parts, (slope_ref, w_ref, out_ref, shifted) = refs[:count], refs[count:]

        @pl.when(lax.axis_index("section") == lax.axis_size("section") - 1 - step)
        def _():
            grad = parts[0][...].astype(F32)
            for part in parts[1:]:
                grad += part[...].astype(F32)
            local = (grad * slope_ref[...]).astype(BF16).astype(F32)
            out_ref[...] = gradient_in(grad, local, shifted, w_ref, rows, cols).astype(BF16)

    return pl.pallas_call(
        kernel,
        out_shape=jax.ShapeDtypeStruct((length, width), BF16),
        in_specs=[VMEM] * (count + 2),
        out_specs=VMEM,
        scratch_shapes=[pltpu.VMEM((3, length + 2 * cols, width), BF16)],
        compiler_params=params_of(),
        cost_estimate=product_cost(weight * taps, length, width, 2 * weights.size),
        name="stage",
    )(*arrived, slope, weights)


def turned_taps(inputs, rows, cols):
    blocks, length, width = inputs.shape

    def kernel(x_ref, out_ref, shifted):
        for n in range(blocks):
            spread(shifted, (), x_ref[n].astype(F32), rows, cols)
            for a in range(3):
                for b in range(3):
                    out_ref[n, 3 * a + b] = shifted[b, a * cols : a * cols + length, :].T

    return pl.pallas_call(
        kernel,
        out_shape=jax.ShapeDtypeStruct((blocks, 9, width, length), BF16),
        in_specs=[VMEM],
        out_specs=VMEM,
        scratch_shapes=[pltpu.VMEM((3, length + 2 * cols, width), BF16)],
        compiler_params=params_of(),
        name="turned_taps",
    )(inputs)


def outgoing(inputs, near, far, momentum, last, replicas):
    taps, width, _ = near.shape
    share = momentum.shape[1]
    head = inputs.shape[0] * inputs.shape[1]

    def kernel(x_ref, near_ref, far_ref, own_ref, out_ref, rest_ref, total):
        for m in range(inputs.shape[0]):
            out_ref[m * inputs.shape[1] : (m + 1) * inputs.shape[1]] = x_ref[m]
        here = lax.axis_index("replica")
        own_rows = pl.ds(pl.multiple_of(here * share, share), share)
        other_rows = pl.ds(pl.multiple_of(jnp.bitwise_xor(here, last) * share, share), share)
        for k in range(taps):
            total[k % 2] = near_ref[k].astype(F32) + far_ref[k].astype(F32)
            mine = total[k % 2, own_rows, :]
            at = head + k * 2 * share
            out_ref[at : at + share] = (1.33 / replicas * mine + 0.567 * own_ref[k]).astype(BF16)
            out_ref[at + share : at + 2 * share] = total[k % 2, other_rows, :].astype(BF16)
            rest_ref[k] = 0.9 * own_ref[k] + mine / replicas

    return pl.pallas_call(
        kernel,
        out_shape=(
            jax.ShapeDtypeStruct((head + taps * 2 * share, width), BF16),
            jax.ShapeDtypeStruct(momentum.shape, F32),
        ),
        in_specs=[VMEM] * 4,
        out_specs=[VMEM] * 2,
        scratch_shapes=[pltpu.VMEM((2, width, width), F32)],
        compiler_params=params_of(),
        name="outgoing",
    )(inputs, near, far, momentum)


def incoming(ours, theirs, rest, replicas):
    taps, share, width = rest.shape
    head = ours.shape[0] - taps * 2 * share

    def kernel(ours_ref, theirs_ref, rest_ref, out_ref, momentum_ref):
        for k in range(taps):
            lines = slice(head + k * 2 * share, head + (k + 1) * 2 * share)
            mine, there = ours_ref[lines].astype(F32), theirs_ref[lines].astype(F32)
            out_ref[k, :share] = (mine[:share] + 1.33 / replicas * there[share:]).astype(BF16)
            out_ref[k, share:] = (there[:share] + 1.33 / replicas * mine[share:]).astype(BF16)
            momentum_ref[k] = rest_ref[k] + there[share:] / replicas

    return pl.pallas_call(
        kernel,
        out_shape=(jax.ShapeDtypeStruct((taps, 2 * share, width), BF16), jax.ShapeDtypeStruct(rest.shape, F32)),
        in_specs=[VMEM] * 3,
        out_specs=[VMEM] * 2,
        compiler_params=params_of(),
        name="incoming",
    )(ours, theirs, rest)


def contract(base, momentum_base, blocks, gains, final, pieces=(), last=0, cost=0, grid=(0, 0)):
    taps, width, _ = base.shape
    share = momentum_base.shape[1]
    count = len(blocks)

    def kernel(base_ref, mom_ref, *refs):
        turned, local, refs = refs[:count], refs[count : 2 * count], refs[2 * count :]
        taken, refs = refs[: len(pieces)], refs[len(pieces) :]
        out_ref, mom_out_ref, total = refs[:3]
        if final:
            out_now, mom_now, sems, shifted = refs[3:]
            for n, (one, m, _) in enumerate(blocks):
                if one.ndim == 3:
                    spread(shifted, (n,), turned[n][m].astype(F32), *grid)
        else:
            out_now, mom_now = out_ref, mom_out_ref
        here = lax.axis_index("replica")
        own = pl.multiple_of(here * share, share)
        copies = []
        for k in range(taps):
            acc = None
            for n in range(count):
                if blocks[n][0].ndim == 3:
                    first = k // 3 * grid[1]
                    left = shifted[n, k % 3, first : first + grid[0] * grid[1], :].T
                else:
                    left = turned[n][blocks[n][1], k]
                term = lax.dot_general(left, local[n][...], NN, preferred_element_type=F32)
                acc = term if acc is None else acc + term
            total[k % 2] = acc
            out_now[k] = base_ref[k] + gains[0] * acc
            for (at, low_tap, _), piece in zip(pieces, taken):
                j = k - low_tap
                for n in range(2 if 0 <= j < piece.shape[0] else 0):
                    where = jnp.bitwise_xor(here, at | n * last) * share
                    lines = pl.ds(pl.multiple_of(where, share), share)
                    out_now[k, lines, :] -= piece[j, n * share : (n + 1) * share].astype(F32)
            mom_now[k] = mom_ref[k] + gains[1] * total[k % 2, pl.ds(own, share), :]
            if final:
                copies.append(pltpu.make_async_copy(out_now.at[k], out_ref.at[k], sems.at[0, k]))
                copies.append(pltpu.make_async_copy(mom_now.at[k], mom_out_ref.at[k], sems.at[1, k]))
                copies[-2].start()
                copies[-1].start()
        for copy in copies:
            copy.wait()

    scratch = [pltpu.VMEM((2, width, width), F32)]
    if final:
        scratch += [
            pltpu.VMEM(base.shape, F32),
            pltpu.VMEM(momentum_base.shape, F32),
            pltpu.SemaphoreType.DMA((2, taps)),
            pltpu.VMEM((count, 3, (grid[0] + 2) * grid[1], width), BF16),
        ]
    return pl.pallas_call(
        kernel,
        out_shape=(
            jax.ShapeDtypeStruct(base.shape, F32),
            jax.ShapeDtypeStruct(momentum_base.shape, F32),
        ),
        in_specs=[VMEM] * (2 + 2 * count + len(pieces)),
        out_specs=[HBM if final else VMEM] * 2,
        scratch_shapes=scratch,
        compiler_params=params_of(),
        cost_estimate=pl.CostEstimate(flops=cost, bytes_accessed=0, transcendentals=0),
        name="contract",
    )(base, momentum_base, *[one[0] for one in blocks], *[one[2] for one in blocks], *[one[2] for one in pieces])


def per_device(section_inputs, cotangent, crop_rows, drift, params, momentum):
    sections = lax.axis_size("section")
    here, replicas = lax.axis_index("replica"), lax.axis_size("replica")
    micro, rows, cols, width = section_inputs.shape[2:]
    length = rows * cols
    share = width // replicas
    taps = params.shape[1]
    scale = (9.0 * width) ** (-0.5)
    bits = [1 << n for n in reversed(range((replicas - 1).bit_length()))]
    x = section_inputs.reshape(micro, length, width)
    cot = cotangent.reshape(micro, length, width)

    def swap(value, bit):
        return lax.ppermute(value, "replica", [(i, i ^ bit) for i in range(replicas)])

    def spread_out(value, through):
        held = [(0, value)]
        for bit in through:
            held += [(at | bit, swap(one, bit)) for at, one in held]
        return held

    def hop(value, step):
        return lax.ppermute(value, "section", [(sections - 1 - step, sections - 2 - step)])

    def slice_of(value, relative):
        at = jnp.bitwise_xor(here, relative) * share
        return lax.dynamic_slice_in_dim(value, at, share, 1).astype(F32)

    low, last = bits[1:], bits[0]
    own, near = momentum[0], drift[0, 0]
    far = swap(near, 1) if low else jnp.zeros_like(near)
    weights, x_near, slopes, tops = prepare(crop_rows, x, cot, params[0], rows, cols)
    arrived = [[top] for top in tops]
    for step in range(sections - 1):
        hints = [LATER_WEIGHT if step else STAGE_WEIGHT] * micro
        hints[0] = hints[0] if step else FIRST_WEIGHT
        leaving = [stage(step, arrived[m], slopes[m], weights, rows, cols, hints[m]) for m in range(micro)]
        for m in range(micro):
            arrived[m].append(hop(leaving[m], step))
        if step == 0:
            far, x_sent = after(far, *leaving), after(x_near, *leaving)
            if len(low) < 2:
                ours, rest = outgoing(x_sent, near, far, own, last, replicas)
            else:
                live = {j: slice_of(near, j) + slice_of(far, j) for j in range(0, replicas, 2)}
                for bit in reversed(low[:-1]):
                    got = {j: swap(v.astype(BF16), bit) for j, v in live.items() if j & bit}
                    live = {j: v + got[j | bit].astype(F32) for j, v in live.items() if not j & bit}
                ours = jnp.concatenate([1.33 / replicas * live[0] + 0.567 * own, live[last]], axis=1).astype(BF16)
                ours = jnp.concatenate([x_sent.reshape(-1, width), ours.reshape(-1, width)])
                rest = 0.9 * own + live[0] / replicas
        arrived[0][-1] = after(arrived[0][-1], *leaving[1:], *([ours] if step == 0 else []))
    theirs = swap(ours, last)


    x_there = theirs[: micro * length].reshape(x.shape)
    turned = {at: turned_taps(one, rows, cols) for at, one in spread_out(x_sent, low)}
    x_far = spread_out(x_there, low)
    turned |= {at | last: one if replicas <= 4 and at == 0 else turned_taps(one, rows, cols) for at, one in x_far}
    gain = 0.5 * scale / replicas
    gains = (-1.33 * gain, gain)
    arrived[0][-1] = after(arrived[0][-1], *[one for at, one in turned.items() if at < last])
    near, crossed = [], []
    for m in range(micro):
        local = (sum(one.astype(F32) for one in arrived[m]) * slopes[m]).astype(BF16)
        crossed.append(swap(local, last))
        near.append([(turned[at], m, one) for at, one in spread_out(local, low)])
    base, momentum_base = params[0], rest
    for m in range(micro):
        if m:
            at, _, one = near[m][-1]
            near[m][-1] = (at, m, after(one, base))
        else:
            base = after(base, crossed[0])
        base, momentum_base = contract(base, momentum_base, near[m], gains, False, cost=CONTRACT_COST)
        if m == 0:
            pair, momentum_base = incoming(ours, theirs, momentum_base, replicas)
    blocks = []
    for m in range(micro):
        blocks += [(turned[at | last], m, one) for at, one in spread_out(after(crossed[m], base), low)]
    pieces = []
    for k in range(0, taps, 3):
        pieces += [(at, k, one) for at, one in spread_out(pair[k : k + 3], low)]
    for at in range(0, len(blocks), 4):
        end = at + 4 >= len(blocks)
        base, momentum_base = contract(
            base, momentum_base, blocks[at : at + 4], gains, end, pieces, last, grid=(rows, cols)
        )
        pieces = ()
    return (base[None], momentum_base[None])


def solution(mesh):
    placed = (
        P(("groups", "replica"), "section", None, None, None, None),
        P(("groups", "replica"), None, None, None, None),
        P(("groups", "replica"), None),
        P(("groups", "replica"), "section", None, None, None),
        P(("groups", "section"), None, None, None),
        P(("groups", "section"), None, "replica", None),
    )
    return jax.shard_map(
        per_device,
        mesh=mesh,
        in_specs=placed,
        out_specs=(
            P(("groups", "section"), None, None, None),
            P(("groups", "section"), None, "replica", None),
        ),
        check_vma=False,
    )
```
